32 devices in a mesh: mode: 4 (over z), samp: 4 (over x, core), pts: 2 (over y).
Axes of the slice: x: 2, y: 2, z: 4, core: 2. Of those that a mesh axis runs over, the one named last changes fastest.
Arguments:
- coefficients: bfloat16 [768, 12288], P('samp', 'mode'), may hold values from -15 to 15
- panels: bfloat16 [12288, 16384], P(('mode', 'samp'), 'pts'), may hold values from -0.02734375 to 0.02734375
- mean_field: float32 [16384], P('pts'), may hold values from -3 to 3
- load: float32 [16384], P('pts'), may hold values from 0.5 to 2
Outputs:
- standardized: float32 [768], P('samp')
The draws below stay inside these ranges and needn't reach their ends.
All inputs are finite; a program needn't handle non-finite values.
Results may differ from the reference program's by a relative error of at most 0.0003.
Values may be sent and summed in bfloat16 or wider, within the bound.
A program may use at most 128 MiB of HBM per device.

```python
import math
import jax
import jax.numpy as jnp
from jax import lax

POINTS = 16384
MODES = 12288
SAMPLES = 768


def draw_coefficients(key, part):
    first = jax.random.fold_in(key, 11)
    rows = jnp.arange(SAMPLES).astype(jnp.float32)
    scaling = 3.0 ** (rows / (SAMPLES - 1))
    values = jax.random.truncated_normal(first, -4.0, 4.0, (SAMPLES, MODES), jnp.float32)
    return (values * scaling[:, None]).astype(jnp.bfloat16)


def steps_of(stream_key, dims, pieces, least, high):
    factor_of, own = 1.0, jax.random.fold_in(stream_key, 6)
    for axis_at, shards_of in pieces:
        heights = jnp.exp(jax.random.uniform(jax.random.fold_in(own, axis_at), (shards_of,), jnp.float32, least / len(pieces), high / len(pieces)))
        factor_of = factor_of * jnp.repeat(heights, dims[axis_at] // shards_of).reshape([-1 if axis == axis_at else 1 for axis in range(len(dims))])
    return factor_of


def scatter_about(stream_key, shape, deviation, bound, cuts=(), dtype=jnp.bfloat16):
    values = jax.random.normal(stream_key, shape, jnp.float32) * deviation
    if len(cuts) > 0:
        values = steps_of(stream_key, shape, cuts, -0.22, 0.18) * values
    return jnp.clip(values, min=-bound, max=bound).astype(dtype)


def setup_inputs(seed: int = 0) -> dict:
    key_of = jax.random.split(jax.random.key(seed), 5)
    return {
        "coefficients": draw_coefficients(jax.random.fold_in(key_of[4], 71), 0),
        "panels": scatter_about(key_of[1], (MODES, POINTS), (4 * MODES) ** -0.5, 0.02734375, ((0, 16), (1, 2))),
        "mean_field": scatter_about(key_of[2], (POINTS,), 0.5, 3.0, ((0, 2),), jnp.float32),
        "load": jnp.clip(jnp.exp(math.log(2.0) - 1.3862944 * jax.random.uniform(key_of[3], (POINTS,), jnp.float32) ** steps_of(key_of[3], (POINTS,), ((0, 2),), -0.2, 0.2)), 0.5, 2.0),
    }


def reference(coefficients, panels, mean_field, load):
    field = jnp.dot(coefficients, panels, preferred_element_type=jnp.float32) + mean_field[None, :]
    weighted = load[None, :] * jnp.exp(field)
    fine_qoi = lax.optimization_barrier(jnp.sum(weighted, axis=1)) / POINTS
    coarse_qoi = lax.optimization_barrier(jnp.sum(weighted[:, ::2], axis=1)) * (2.0 / POINTS)
    level_diff = fine_qoi - coarse_qoi
    center = jnp.sum(level_diff) / SAMPLES
    spread = jnp.sum((level_diff - center) ** 2) / SAMPLES
    return (level_diff - center) / jnp.sqrt(spread + 1e-06)
```

```python
import jax
import jax.numpy as jnp
from jax import lax
from jax.sharding import PartitionSpec as P


def body(points, coefficients, panels, mean_field, load):
    rows = lax.all_gather(coefficients, "samp", axis=0, tiled=True)
    mine = lax.all_to_all(panels, "samp", split_axis=1, concat_axis=0, tiled=True)
    partial_value = jnp.dot(rows, mine, preferred_element_type=jnp.float32)
    portion = lax.psum_scatter(partial_value, "mode", scatter_dimension=1, tiled=True)
    count = portion.shape[1]
    offset = lax.axis_index("samp") * mine.shape[1] + lax.axis_index("mode") * count
    local_mean = lax.dynamic_slice_in_dim(mean_field, offset, count, 0)
    local_load = lax.dynamic_slice_in_dim(load, offset, count, 0)
    weighted = local_load[None, :] * jnp.exp(portion + local_mean[None, :])
    even = (lax.broadcasted_iota(jnp.int32, (1, count), 1) % 2) == 0
    fine = jnp.sum(weighted, axis=1)
    coarse = jnp.sum(jnp.where(even, weighted, 0.0), axis=1)
    fine, coarse = lax.psum((fine, coarse), ("mode", "samp", "pts"))
    level_diff = fine / points - coarse * (2.0 / points)
    total = level_diff.shape[0]
    center = jnp.sum(level_diff) / total
    shifted = level_diff - center
    spread = jnp.sum(shifted * shifted) / total
    out = shifted / jnp.sqrt(spread + 1e-06)
    own = coefficients.shape[0]
    return lax.dynamic_slice_in_dim(out, lax.axis_index("samp") * own, own, 0)


def solution(mesh):
    in_specs = (P("samp", "mode"), P(("mode", "samp"), "pts"), P("pts"), P("pts"))

    def run(coefficients, panels, mean_field, load):
        def inner(*args):
            return body(mean_field.shape[0], *args)

        return jax.shard_map(inner, mesh=mesh, in_specs=in_specs, out_specs=P("samp"), check_vma=False)(
            coefficients, panels, mean_field, load
        )

    return run
```

```python
import functools

import jax
import jax.numpy as jnp
from jax import lax
from jax.experimental import pallas as pl
from jax.experimental.pallas import tpu as pltpu
from jax.sharding import PartitionSpec as P

MESH = pl.DeviceIdType.MESH
WIDTH = 256
LANES = 128


def kernel(
    depth, chunks, coef_hbm, panel_hbm, mean_ref, load_ref, acc_ref,
    coef, panel, out, core_in, cross_in, line_in_x, line_in_z,
    coef_send, coef_recv, coef_local, panel_sem,
    core_send, core_recv, cross_send, cross_recv, line_send, line_recv,
):
    samp, line = lax.axis_index("samp"), lax.axis_index("mode")
    length = lax.axis_size("mode")
    last = length - 1
    rows = coef_hbm.shape[0]
    partner = samp + 1 - 2 * lax.rem(samp, 2)
    across = lax.rem(samp + 2, 4)
    diagonal = lax.rem(partner + 2, 4)
    peers = (across, partner, diagonal)

    barrier = pltpu.get_barrier_semaphore()
    for peer in peers:
        pl.semaphore_signal(barrier, inc=1, device_id={"samp": peer}, device_id_type=MESH)
    for peer in (lax.rem(line + 1, length), lax.rem(line + last, length)):
        pl.semaphore_signal(barrier, inc=1, device_id={"mode": peer}, device_id_type=MESH)
    pl.semaphore_wait(barrier, 5)

    def panel_copy(j):
        slot = lax.rem(j, 2)
        columns = pl.ds(pl.multiple_of(j * WIDTH, WIDTH), WIDTH)
        return pltpu.make_async_copy(panel_hbm.at[:, columns], panel.at[slot], panel_sem.at[slot])

    def coef_copy(i):
        columns = pl.ds(pl.multiple_of(peers[i] * depth, depth), depth)
        return pltpu.make_async_remote_copy(
            coef_hbm.at[:, columns], coef.at[pl.ds((i + 1) * rows, rows), :],
            coef_send.at[i], coef_recv.at[i], device_id={"samp": peers[i]}, device_id_type=MESH,
        )

    for i in (0, 2, 1):
        coef_copy(i).start()
    own = pltpu.make_async_copy(
        coef_hbm.at[:, pl.ds(pl.multiple_of(samp * depth, depth), depth)], coef.at[pl.ds(0, rows), :], coef_local
    )
    own.start()
    panel_copy(0).start()
    acc_ref[...] = jnp.zeros_like(acc_ref)

    def core_copy(j):
        return pltpu.make_async_remote_copy(
            out.at[j, pl.ds(2 * rows, 2 * rows), :], core_in.at[j],
            core_send.at[j], core_recv.at[j], device_id={"samp": partner}, device_id_type=MESH,
        )

    def cross_copy(j):
        return pltpu.make_async_remote_copy(
            out.at[j, pl.ds(rows, rows), :], cross_in.at[j],
            cross_send.at[j], cross_recv.at[j], device_id={"samp": across}, device_id_type=MESH,
        )

    def up(j):
        return lax.rem(j // 2, 2)

    def place(j):
        return up(j) * line + (1 - up(j)) * (last - line)

    def line_copy(j, kind):
        size = (1 + kind) * rows
        into = line_in_z if kind else line_in_x
        target = lax.rem(line + 2 * up(j) - 1 + length, length)
        return pltpu.make_async_remote_copy(
            out.at[j, pl.ds(0, size), :], into.at[j // 2],
            line_send.at[j], line_recv.at[j], device_id={"mode": target}, device_id_type=MESH,
        )

    def finish(j, field):
        columns = pl.ds(pl.multiple_of(j * WIDTH, WIDTH), WIDTH)
        weighted = load_ref[:, columns] * jnp.exp(field + mean_ref[:, columns])
        total = acc_ref[...]
        for at in range(0, WIDTH, LANES):
            total = total + weighted[:, at : at + LANES]
        acc_ref[...] = total

    def begin(j):
        @pl.when(j + 1 < chunks)
        def _():
            panel_copy(j + 1).start()

        panel_copy(j).wait()
        out[j] = jnp.dot(coef[...], panel[lax.rem(j, 2)], preferred_element_type=jnp.float32)
        core_copy(j).start()

    def joined(j):
        core_copy(j).wait_recv()
        out[j, pl.ds(0, 2 * rows), :] += core_in[j]

        @pl.when(lax.rem(j, 2) == 0)
        def _():
            cross_copy(j).start()

        @pl.when((lax.rem(j, 2) == 1) & (place(j) == 0))
        def _():
            line_copy(j, 1).start()

    def crossed(j):
        cross_copy(j).wait_recv()
        out[j, pl.ds(0, rows), :] += cross_in[j]

        @pl.when(place(j) == 0)
        def _():
            line_copy(j, 0).start()

    def hop(j, kind, at):
        @pl.when(place(j) == at)
        def _():
            line_copy(j, kind).wait_recv()
            if at < last:
                out[j, pl.ds(0, (1 + kind) * rows), :] += (line_in_z if kind else line_in_x)[j // 2]
                line_copy(j, kind).start()
            elif kind:
                out[j, pl.ds(0, 2 * rows), :] += line_in_z[j // 2]
                cross_copy(j).start()
            else:
                finish(j, out[j, pl.ds(0, rows), :] + line_in_x[j // 2])

    def back(j):
        @pl.when(place(j) == last)
        def _():
            cross_copy(j).wait_recv()
            finish(j, out[j, pl.ds(0, rows), :] + cross_in[j])

    own.wait()
    for i in range(3):
        coef_copy(i).wait()

    stages = [(0, None, begin), (1, None, joined), (1 + CROSS_LAG, 0, crossed)]
    for at in range(1, last + 1):
        stages.append((1 + CROSS_LAG + LINE_LAG * at, 0, functools.partial(hop, kind=0, at=at)))
        stages.append((1 + WIDE_LAG * at, 1, functools.partial(hop, kind=1, at=at)))
    stages.append((1 + WIDE_LAG * last + CROSS_LAG, 1, back))
    end = max(lag for lag, _, _ in stages)

    def tick(t, carry):
        for lag, kind, stage in stages:
            j = t - lag
            here = (j >= 0) & (j < chunks)
            if kind is not None:
                here = here & (lax.rem(j + 2 * end, 2) == kind)
            pl.when(here)(functools.partial(stage, j))
        return carry

    lax.fori_loop(0, chunks + end, tick, 0)

    def drain(j, carry):
        core_copy(j).wait_send()
        even, final = lax.rem(j, 2) == 0, place(j) == last

        @pl.when(even | final)
        def _():
            cross_copy(j).wait_send()

        @pl.when(even & (place(j) < last))
        def _():
            line_copy(j, 0).wait_send()

        @pl.when((lax.rem(j, 2) == 1) & (place(j) < last))
        def _():
            line_copy(j, 1).wait_send()

        return carry

    lax.fori_loop(0, chunks, drain, 0)


CROSS_LAG, LINE_LAG, WIDE_LAG = 3, 2, 4


def lane_sums(coefficients, panels, mean_field, load):
    rows = coefficients.shape[0]
    depth, points = panels.shape
    chunks = points // WIDTH
    every = pl.BlockSpec(memory_space=pl.ANY)
    here = pl.BlockSpec(memory_space=pltpu.VMEM)
    dma = pltpu.SemaphoreType.DMA
    f32 = jnp.float32
    return pl.pallas_call(
        functools.partial(kernel, depth, chunks),
        out_shape=jax.ShapeDtypeStruct((rows, LANES), f32),
        in_specs=[every, every, here, here],
        out_specs=here,
        scratch_shapes=[
            pltpu.VMEM((4 * rows, depth), jnp.bfloat16),
            pltpu.VMEM((2, depth, WIDTH), jnp.bfloat16),
            pltpu.VMEM((chunks, 4 * rows, WIDTH), f32),
            pltpu.VMEM((chunks, 2 * rows, WIDTH), f32),
            pltpu.VMEM((chunks, rows, WIDTH), f32),
            pltpu.VMEM((chunks // 2, rows, WIDTH), f32),
            pltpu.VMEM((chunks // 2, 2 * rows, WIDTH), f32),
            dma((3,)), dma((3,)), dma, dma((2,)),
            dma((chunks,)), dma((chunks,)), dma((chunks,)), dma((chunks,)), dma((chunks,)), dma((chunks,)),
        ],
        compiler_params=pltpu.CompilerParams(
            collective_id=0, has_side_effects=True, vmem_limit_bytes=67043328
        ),
    )(coefficients, panels, mean_field[None, :], load[None, :])


def lined(points, coefficients, panels, mean_field, load):
    sums = lane_sums(coefficients, panels, mean_field, load)
    even = (lax.broadcasted_iota(jnp.int32, (1, LANES), 1) % 2) == 0
    parts = jnp.sum(sums, axis=1), jnp.sum(jnp.where(even, sums, 0.0), axis=1)
    fine, coarse = lax.psum(parts, ("mode", "pts"))
    level_diff = fine / points - coarse * (2.0 / points)
    total = level_diff.shape[0] * lax.axis_size("samp")
    center = lax.psum(jnp.sum(level_diff), "samp") / total
    shifted = level_diff - center
    spread = lax.psum(jnp.sum(shifted * shifted), "samp") / total
    return shifted / jnp.sqrt(spread + 1e-06)


def gathered(points, coefficients, panels, mean_field, load):
    rows = lax.all_gather(coefficients, "samp", axis=0, tiled=True)
    mine = lax.all_to_all(panels, "samp", split_axis=1, concat_axis=0, tiled=True)
    partial_value = jnp.dot(rows, mine, preferred_element_type=jnp.float32)
    portion = lax.psum_scatter(partial_value, "mode", scatter_dimension=1, tiled=True)
    count = portion.shape[1]
    offset = lax.axis_index("samp") * mine.shape[1] + lax.axis_index("mode") * count
    local_mean = lax.dynamic_slice_in_dim(mean_field, offset, count, 0)
    local_load = lax.dynamic_slice_in_dim(load, offset, count, 0)
    weighted = local_load[None, :] * jnp.exp(portion + local_mean[None, :])
    even = (lax.broadcasted_iota(jnp.int32, (1, count), 1) % 2) == 0
    fine = jnp.sum(weighted, axis=1)
    coarse = jnp.sum(jnp.where(even, weighted, 0.0), axis=1)
    fine, coarse = lax.psum((fine, coarse), ("mode", "samp", "pts"))
    level_diff = fine / points - coarse * (2.0 / points)
    total = level_diff.shape[0]
    center = jnp.sum(level_diff) / total
    shifted = level_diff - center
    spread = jnp.sum(shifted * shifted) / total
    out = shifted / jnp.sqrt(spread + 1e-06)
    own = coefficients.shape[0]
    return lax.dynamic_slice_in_dim(out, lax.axis_index("samp") * own, own, 0)


def solution(mesh):
    in_specs = (P("samp", "mode"), P(("mode", "samp"), "pts"), P("pts"), P("pts"))

    def run(coefficients, panels, mean_field, load):
        def inner(*args):
            form = lined if mesh.shape["samp"] == 4 and mesh.shape["mode"] > 2 else gathered
            return form(mean_field.shape[0], *args)

        return jax.shard_map(inner, mesh=mesh, in_specs=in_specs, out_specs=P("samp"), check_vma=False)(
            coefficients, panels, mean_field, load
        )

    return run
```

```python
import functools

import jax
import jax.numpy as jnp
from jax import lax
from jax.experimental import pallas as pl
from jax.experimental.pallas import tpu as pltpu
from jax.sharding import PartitionSpec as P

MESH = pl.DeviceIdType.MESH
WIDTH = 256
LANES = 128


def kernel(
    depth, chunks, points, coef_hbm, panel_hbm, mean_ref, load_ref, result_ref,
    acc_ref, parts, parts_in, diffs, diffs_in, coef, panel, out, core_in, cross_in, line_in_x, line_in_z,
    coef_send, coef_recv, coef_local, panel_sem,
    core_send, core_recv, cross_send, cross_recv, line_send, line_recv,
    parts_send, parts_recv, diffs_send, diffs_recv,
):
    samp, line = lax.axis_index("samp"), lax.axis_index("mode")
    length = lax.axis_size("mode")
    last = length - 1
    rows = coef_hbm.shape[0]
    partner = samp + 1 - 2 * lax.rem(samp, 2)
    across = lax.rem(samp + 2, 4)
    diagonal = lax.rem(partner + 2, 4)
    peers = (across, partner, diagonal)

    barrier = pltpu.get_barrier_semaphore()
    for peer in peers:
        pl.semaphore_signal(barrier, inc=1, device_id={"samp": peer}, device_id_type=MESH)
    side, sides = lax.axis_index("pts"), lax.axis_size("pts")
    group = []
    for on in range(length * sides):
        if on > 0:
            group.append((lax.rem(line + on // sides, length), lax.rem(side + on % sides, sides)))
    for there, beside in group:
        pl.semaphore_signal(barrier, inc=1, device_id={"mode": there, "pts": beside}, device_id_type=MESH)
    pl.semaphore_wait(barrier, 3 + len(group))

    def panel_copy(j):
        slot = lax.rem(j, 2)
        columns = pl.ds(pl.multiple_of(j * WIDTH, WIDTH), WIDTH)
        return pltpu.make_async_copy(panel_hbm.at[:, columns], panel.at[slot], panel_sem.at[slot])

    def coef_copy(i):
        columns = pl.ds(pl.multiple_of(peers[i] * depth, depth), depth)
        return pltpu.make_async_remote_copy(
            coef_hbm.at[:, columns], coef.at[pl.ds((i + 1) * rows, rows), :],
            coef_send.at[i], coef_recv.at[i], device_id={"samp": peers[i]}, device_id_type=MESH,
        )

    for i in (0, 2, 1):
        coef_copy(i).start()
    own = pltpu.make_async_copy(
        coef_hbm.at[:, pl.ds(pl.multiple_of(samp * depth, depth), depth)], coef.at[pl.ds(0, rows), :], coef_local
    )
    own.start()
    panel_copy(0).start()
    acc_ref[...] = jnp.zeros_like(acc_ref)

    def core_copy(j):
        return pltpu.make_async_remote_copy(
            out.at[j, pl.ds(2 * rows, 2 * rows), :], core_in.at[j],
            core_send.at[j], core_recv.at[j], device_id={"samp": partner}, device_id_type=MESH,
        )

    def cross_copy(j):
        return pltpu.make_async_remote_copy(
            out.at[j, pl.ds(rows, rows), :], cross_in.at[j],
            cross_send.at[j], cross_recv.at[j], device_id={"samp": across}, device_id_type=MESH,
        )

    def up(j):
        return lax.rem(j // 2, 2)

    def place(j):
        return up(j) * line + (1 - up(j)) * (last - line)

    def line_copy(j, kind):
        size = (1 + kind) * rows
        into = line_in_z if kind else line_in_x
        target = lax.rem(line + 2 * up(j) - 1 + length, length)
        return pltpu.make_async_remote_copy(
            out.at[j, pl.ds(0, size), :], into.at[j // 2],
            line_send.at[j], line_recv.at[j], device_id={"mode": target}, device_id_type=MESH,
        )

    def finish(j, field):
        columns = pl.ds(pl.multiple_of(j * WIDTH, WIDTH), WIDTH)
        weighted = load_ref[:, columns] * jnp.exp(field + mean_ref[:, columns])
        total = acc_ref[pl.ds(0, rows), :]
        for at in range(0, WIDTH, LANES):
            total = total + weighted[:, at : at + LANES]
        acc_ref[pl.ds(0, rows), :] = total

    def begin(j):
        @pl.when(j + 1 < chunks)
        def _():
            panel_copy(j + 1).start()

        panel_copy(j).wait()
        out[j] = jnp.dot(coef[...], panel[lax.rem(j, 2)], preferred_element_type=jnp.float32)
        core_copy(j).start()

    def joined(j):
        core_copy(j).wait_recv()
        out[j, pl.ds(0, 2 * rows), :] += core_in[j]

        @pl.when(lax.rem(j, 2) == 0)
        def _():
            cross_copy(j).start()

        @pl.when((lax.rem(j, 2) == 1) & (place(j) == 0))
        def _():
            line_copy(j, 1).start()

    def crossed(j):
        cross_copy(j).wait_recv()
        out[j, pl.ds(0, rows), :] += cross_in[j]

        @pl.when(place(j) == 0)
        def _():
            line_copy(j, 0).start()

    def hop(j, kind, at):
        @pl.when(place(j) == at)
        def _():
            line_copy(j, kind).wait_recv()
            if at < last:
                out[j, pl.ds(0, (1 + kind) * rows), :] += (line_in_z if kind else line_in_x)[j // 2]
                line_copy(j, kind).start()
            elif kind:
                out[j, pl.ds(0, 2 * rows), :] += line_in_z[j // 2]
                cross_copy(j).start()
            else:
                finish(j, out[j, pl.ds(0, rows), :] + line_in_x[j // 2])

    def back(j):
        @pl.when(place(j) == last)
        def _():
            cross_copy(j).wait_recv()
            finish(j, out[j, pl.ds(0, rows), :] + cross_in[j])

    own.wait()
    for i in range(3):
        coef_copy(i).wait()

    stages = [(0, None, begin), (1, None, joined), (1 + CROSS_LAG, 0, crossed)]
    for at in range(1, last + 1):
        stages.append((1 + CROSS_LAG + LINE_LAG * at, 0, functools.partial(hop, kind=0, at=at)))
        stages.append((1 + WIDE_LAG * at, 1, functools.partial(hop, kind=1, at=at)))
    stages.append((1 + WIDE_LAG * last + CROSS_LAG, 1, back))
    end = max(lag for lag, _, _ in stages)

    def tick(t, carry):
        for lag, kind, stage in stages:
            j = t - lag
            here = (j >= 0) & (j < chunks)
            if kind is not None:
                here = here & (lax.rem(j + 2 * end, 2) == kind)
            pl.when(here)(functools.partial(stage, j))
        return carry

    lax.fori_loop(0, chunks + end, tick, 0)

    per_lane = acc_ref[...].T
    even = lax.rem(lax.broadcasted_iota(jnp.int32, per_lane.shape, 0), 2) == 0
    fine_part = jnp.sum(per_lane, axis=0, keepdims=True)
    coarse_part = jnp.sum(jnp.where(even, per_lane, 0.0), axis=0, keepdims=True)
    sublane = lax.broadcasted_iota(jnp.int32, parts.shape, 0)
    parts[...] = jnp.where(sublane == 0, fine_part, jnp.where(sublane == 1, coarse_part, 0.0))
    is_end = (line == 0) | (line == last)
    mine = (line // last) * sides + side

    def parts_copy(i, slot):
        there, beside = group[i]
        return pltpu.make_async_remote_copy(
            parts, parts_in.at[slot], parts_send.at[i], parts_recv.at[slot],
            device_id={"mode": there, "pts": beside}, device_id_type=MESH,
        )

    @pl.when(is_end)
    def _():
        for i in range(len(group)):
            parts_copy(i, mine).start()
        parts_in[mine] = parts[...]

    for slot in range(2 * sides):
        @pl.when(jnp.logical_not(is_end & (mine == slot)))
        def _(slot=slot):
            parts_copy(0, slot).wait_recv()

    total = parts_in[0]
    for slot in range(1, 2 * sides):
        total = total + parts_in[slot]
    fine, coarse = total[0:1, :] / points, total[1:2, :] * (2.0 / points)
    diffs[...] = jnp.broadcast_to(fine - coarse, diffs.shape)

    def diffs_copy(i, slot):
        return pltpu.make_async_remote_copy(
            diffs, diffs_in.at[slot], diffs_send.at[i], diffs_recv.at[slot],
            device_id={"samp": peers[i]}, device_id_type=MESH,
        )

    for i in range(3):
        diffs_copy(i, samp).start()
    diffs_in[samp] = diffs[...]
    for slot in range(4):
        @pl.when(samp != slot)
        def _(slot=slot):
            diffs_copy(0, slot).wait_recv()

    inside = lax.broadcasted_iota(jnp.int32, (1, diffs.shape[1]), 1) < rows
    level = [diffs_in[slot][0:1, :] for slot in range(4)]
    summed = level[0] + level[1] + level[2] + level[3]
    center = jnp.sum(jnp.where(inside, summed, 0.0), axis=1, keepdims=True) / (4 * rows)
    squares = [jnp.where(inside, (one - center) * (one - center), 0.0) for one in level]
    spread = jnp.sum(squares[0] + squares[1] + squares[2] + squares[3], axis=1, keepdims=True) / (4 * rows)
    standardized = (diffs[0:1, :] - center) / jnp.sqrt(spread + 1e-06)
    result_ref[...] = standardized[:, 0:rows]

    for i in range(3):
        diffs_copy(i, samp).wait_send()

    @pl.when(is_end)
    def _():
        for i in range(len(group)):
            parts_copy(i, mine).wait_send()

    def drain(j, carry):
        core_copy(j).wait_send()
        even, final = lax.rem(j, 2) == 0, place(j) == last

        @pl.when(even | final)
        def _():
            cross_copy(j).wait_send()

        @pl.when(even & (place(j) < last))
        def _():
            line_copy(j, 0).wait_send()

        @pl.when((lax.rem(j, 2) == 1) & (place(j) < last))
        def _():
            line_copy(j, 1).wait_send()

        return carry

    lax.fori_loop(0, chunks, drain, 0)


CROSS_LAG, LINE_LAG, WIDE_LAG = 3, 2, 4


def lined(points, coefficients, panels, mean_field, load):
    rows = coefficients.shape[0]
    depth, own = panels.shape
    chunks = own // WIDTH
    every = pl.BlockSpec(memory_space=pl.ANY)
    here = pl.BlockSpec(memory_space=pltpu.VMEM)
    dma = pltpu.SemaphoreType.DMA
    f32 = jnp.float32
    length, sides = lax.axis_size("mode"), lax.axis_size("pts")
    padded = pl.cdiv(rows, LANES) * LANES
    result = pl.pallas_call(
        functools.partial(kernel, depth, chunks, points),
        out_shape=jax.ShapeDtypeStruct((1, rows), f32),
        in_specs=[every, every, here, here],
        out_specs=here,
        scratch_shapes=[
            pltpu.VMEM((padded, LANES), f32),
            pltpu.VMEM((8, padded), f32),
            pltpu.VMEM((2 * sides, 8, padded), f32),
            pltpu.VMEM((8, padded), f32),
            pltpu.VMEM((4, 8, padded), f32),
            pltpu.VMEM((4 * rows, depth), jnp.bfloat16),
            pltpu.VMEM((2, depth, WIDTH), jnp.bfloat16),
            pltpu.VMEM((chunks, 4 * rows, WIDTH), f32),
            pltpu.VMEM((chunks, 2 * rows, WIDTH), f32),
            pltpu.VMEM((chunks, rows, WIDTH), f32),
            pltpu.VMEM((chunks // 2, rows, WIDTH), f32),
            pltpu.VMEM((chunks // 2, 2 * rows, WIDTH), f32),
            dma((3,)), dma((3,)), dma, dma((2,)),
            dma((chunks,)), dma((chunks,)), dma((chunks,)), dma((chunks,)), dma((chunks,)), dma((chunks,)),
            dma((length * sides - 1,)), dma((2 * sides,)), dma((3,)), dma((4,)),
        ],
        compiler_params=pltpu.CompilerParams(
            collective_id=0, has_side_effects=True, vmem_limit_bytes=67043328
        ),
    )(coefficients, panels, mean_field[None, :], load[None, :])
    return result[0]


def gathered(points, coefficients, panels, mean_field, load):
    rows = lax.all_gather(coefficients, "samp", axis=0, tiled=True)
    mine = lax.all_to_all(panels, "samp", split_axis=1, concat_axis=0, tiled=True)
    partial_value = jnp.dot(rows, mine, preferred_element_type=jnp.float32)
    portion = lax.psum_scatter(partial_value, "mode", scatter_dimension=1, tiled=True)
    count = portion.shape[1]
    offset = lax.axis_index("samp") * mine.shape[1] + lax.axis_index("mode") * count
    local_mean = lax.dynamic_slice_in_dim(mean_field, offset, count, 0)
    local_load = lax.dynamic_slice_in_dim(load, offset, count, 0)
    weighted = local_load[None, :] * jnp.exp(portion + local_mean[None, :])
    even = (lax.broadcasted_iota(jnp.int32, (1, count), 1) % 2) == 0
    fine = jnp.sum(weighted, axis=1)
    coarse = jnp.sum(jnp.where(even, weighted, 0.0), axis=1)
    fine, coarse = lax.psum((fine, coarse), ("mode", "samp", "pts"))
    level_diff = fine / points - coarse * (2.0 / points)
    total = level_diff.shape[0]
    center = jnp.sum(level_diff) / total
    shifted = level_diff - center
    spread = jnp.sum(shifted * shifted) / total
    out = shifted / jnp.sqrt(spread + 1e-06)
    own = coefficients.shape[0]
    return lax.dynamic_slice_in_dim(out, lax.axis_index("samp") * own, own, 0)


def solution(mesh):
    in_specs = (P("samp", "mode"), P(("mode", "samp"), "pts"), P("pts"), P("pts"))

    def run(coefficients, panels, mean_field, load):
        def inner(*args):
            form = lined if mesh.shape["samp"] == 4 and mesh.shape["mode"] > 2 else gathered
            return form(mean_field.shape[0], *args)

        return jax.shard_map(inner, mesh=mesh, in_specs=in_specs, out_specs=P("samp"), check_vma=False)(
            coefficients, panels, mean_field, load
        )

    return run
```

```python
import functools

import jax
import jax.numpy as jnp
from jax import lax
from jax.experimental import pallas as pl
from jax.experimental.pallas import tpu as pltpu
from jax.sharding import PartitionSpec as P

MESH = pl.DeviceIdType.MESH
WIDTH = 128
PERIOD, WIDE = 2, 1
TAIL = 4
LANES = 128


def kernel(
    depth, chunks, points, coef_hbm, panel_hbm, mean_ref, load_ref, result_ref,
    acc_ref, parts, parts_in, diffs, diffs_in, coef, panel, out, core_in, cross_in, line_in,
    coef_send, coef_recv, coef_local, panel_sem,
    core_send, core_recv, cross_send, cross_recv, line_send, line_recv,
    parts_send, parts_recv, diffs_send, diffs_recv, relay_send, relay_recv,
):
    samp, line = lax.axis_index("samp"), lax.axis_index("mode")
    length = lax.axis_size("mode")
    last = length - 1
    rows = coef_hbm.shape[0]
    partner = samp + 1 - 2 * lax.rem(samp, 2)
    across = lax.rem(samp + 2, 4)
    diagonal = lax.rem(partner + 2, 4)
    peers = (across, partner, diagonal)

    barrier = pltpu.get_barrier_semaphore()
    for peer in peers:
        pl.semaphore_signal(barrier, inc=1, device_id={"samp": peer}, device_id_type=MESH)
    side, sides = lax.axis_index("pts"), lax.axis_size("pts")
    group = []
    for on in range(length * sides):
        if on > 0:
            group.append((lax.rem(line + on // sides, length), lax.rem(side + on % sides, sides)))
    for there, beside in group:
        pl.semaphore_signal(barrier, inc=1, device_id={"mode": there, "pts": beside}, device_id_type=MESH)
    pl.semaphore_wait(barrier, 3 + len(group))

    def panel_copy(j):
        slot = lax.rem(j, 2)
        columns = pl.ds(pl.multiple_of(j * WIDTH, WIDTH), WIDTH)
        return pltpu.make_async_copy(panel_hbm.at[:, columns], panel.at[slot], panel_sem.at[slot])

    half = rows // 2
    mine_half = pl.multiple_of(side * half, half)

    def coef_copy(i):
        columns = pl.ds(pl.multiple_of(peers[i] * depth, depth), depth)
        first, count = (0, rows) if i == 1 else (mine_half, half)
        return pltpu.make_async_remote_copy(
            coef_hbm.at[pl.ds(first, count), columns], coef.at[pl.ds((i + 1) * rows + first, count), :],
            coef_send.at[i], coef_recv.at[i], device_id={"samp": peers[i]}, device_id_type=MESH,
        )

    def coef_relay(i):
        block = coef.at[pl.ds((i + 1) * rows + mine_half, half), :]
        return pltpu.make_async_remote_copy(
            block, block, relay_send.at[i // 2], relay_recv.at[i // 2],
            device_id={"pts": 1 - side}, device_id_type=MESH,
        )

    for i in (0, 2, 1):
        coef_copy(i).start()
    own = pltpu.make_async_copy(
        coef_hbm.at[:, pl.ds(pl.multiple_of(samp * depth, depth), depth)], coef.at[pl.ds(0, rows), :], coef_local
    )
    own.start()
    panel_copy(0).start()
    acc_ref[...] = jnp.zeros_like(acc_ref)

    def core_copy(j):
        return pltpu.make_async_remote_copy(
            out.at[j, pl.ds(2 * rows, 2 * rows), :], core_in.at[j],
            core_send.at[j], core_recv.at[j], device_id={"samp": partner}, device_id_type=MESH,
        )

    def cross_copy(j):
        return pltpu.make_async_remote_copy(
            out.at[j, pl.ds(rows, rows), :], cross_in.at[j],
            cross_send.at[j], cross_recv.at[j], device_id={"samp": across}, device_id_type=MESH,
        )

    def up(j):
        return lax.rem(j // PERIOD, 2)

    def is_wide(j):
        return (lax.rem(j, PERIOD) >= PERIOD - WIDE) & (j < chunks - TAIL)

    def place(j):
        return up(j) * line + (1 - up(j)) * (last - line)

    def line_copy(j, kind):
        size = (1 + kind) * rows
        target = lax.rem(line + 2 * up(j) - 1 + length, length)
        return pltpu.make_async_remote_copy(
            out.at[j, pl.ds(0, size), :], line_in.at[j, pl.ds(0, size), :],
            line_send.at[j], line_recv.at[j], device_id={"mode": target}, device_id_type=MESH,
        )

    def finish(j, field):
        columns = pl.ds(pl.multiple_of(j * WIDTH, WIDTH), WIDTH)
        weighted = load_ref[:, columns] * jnp.exp(field + mean_ref[:, columns])
        total = acc_ref[pl.ds(0, rows), :]
        for at in range(0, WIDTH, LANES):
            total = total + weighted[:, at : at + LANES]
        acc_ref[pl.ds(0, rows), :] = total

    def begin(j):
        @pl.when(j + 1 < chunks)
        def _():
            panel_copy(j + 1).start()

        panel_copy(j).wait()
        out[j] = jnp.dot(coef[...], panel[lax.rem(j, 2)], preferred_element_type=jnp.float32)
        core_copy(j).start()

    def joined(j):
        core_copy(j).wait_recv()
        out[j, pl.ds(0, 2 * rows), :] += core_in[j]

        @pl.when(jnp.logical_not(is_wide(j)))
        def _():
            cross_copy(j).start()

        @pl.when(is_wide(j) & (place(j) == 0))
        def _():
            line_copy(j, 1).start()

    def crossed(j):
        cross_copy(j).wait_recv()
        out[j, pl.ds(0, rows), :] += cross_in[j]

        @pl.when(place(j) == 0)
        def _():
            line_copy(j, 0).start()

    def hop(j, kind, at):
        @pl.when(place(j) == at)
        def _():
            line_copy(j, kind).wait_recv()
            if at < last:
                out[j, pl.ds(0, (1 + kind) * rows), :] += line_in[j, pl.ds(0, (1 + kind) * rows), :]
                line_copy(j, kind).start()
            elif kind:
                out[j, pl.ds(0, 2 * rows), :] += line_in[j]
                cross_copy(j).start()
            else:
                finish(j, out[j, pl.ds(0, rows), :] + line_in[j, pl.ds(0, rows), :])

    def back(j):
        @pl.when(place(j) == last)
        def _():
            cross_copy(j).wait_recv()
            finish(j, out[j, pl.ds(0, rows), :] + cross_in[j])

    own.wait()
    for i in (0, 2):
        coef_copy(i).wait_recv()
        coef_relay(i).start()
    coef_copy(1).wait_recv()
    for i in (0, 2):
        coef_relay(i).wait_recv()

    stages = [(0, None, begin), (JOIN_LAG, None, joined), (JOIN_LAG + CROSS_LAG, 0, crossed)]
    for at in range(1, last + 1):
        stages.append((JOIN_LAG + CROSS_LAG + LINE_LAG * at, 0, functools.partial(hop, kind=0, at=at)))
        stages.append((JOIN_LAG + WIDE_LAG * at, 1, functools.partial(hop, kind=1, at=at)))
    stages.append((JOIN_LAG + WIDE_LAG * last + CROSS_LAG, 1, back))
    end = max(lag for lag, _, _ in stages)

    def tick(t, carry):
        for lag, kind, stage in stages:
            j = t - lag
            here = (j >= 0) & (j < chunks)
            if kind is not None:
                wide = is_wide(j)
                here = here & (wide if kind else jnp.logical_not(wide))
            pl.when(here)(functools.partial(stage, j))
        return carry

    lax.fori_loop(0, chunks + end, tick, 0)

    per_lane = acc_ref[...].T
    even = lax.rem(lax.broadcasted_iota(jnp.int32, per_lane.shape, 0), 2) == 0
    fine_part = jnp.sum(per_lane, axis=0, keepdims=True)
    coarse_part = jnp.sum(jnp.where(even, per_lane, 0.0), axis=0, keepdims=True)
    sublane = lax.broadcasted_iota(jnp.int32, parts.shape, 0)
    parts[...] = jnp.where(sublane == 0, fine_part, jnp.where(sublane == 1, coarse_part, 0.0))
    is_end = (line == 0) | (line == last)
    mine = (line // last) * sides + side

    def parts_copy(i, slot):
        there, beside = group[i]
        return pltpu.make_async_remote_copy(
            parts, parts_in.at[slot], parts_send.at[i], parts_recv.at[slot],
            device_id={"mode": there, "pts": beside}, device_id_type=MESH,
        )

    @pl.when(is_end)
    def _():
        for i in range(len(group)):
            parts_copy(i, mine).start()
        parts_in[mine] = parts[...]

    for slot in range(2 * sides):
        @pl.when(jnp.logical_not(is_end & (mine == slot)))
        def _(slot=slot):
            parts_copy(0, slot).wait_recv()

    total = parts_in[0]
    for slot in range(1, 2 * sides):
        total = total + parts_in[slot]
    fine, coarse = total[0:1, :] / points, total[1:2, :] * (2.0 / points)
    diffs[...] = jnp.broadcast_to(fine - coarse, diffs.shape)

    def diffs_copy(i, slot):
        return pltpu.make_async_remote_copy(
            diffs, diffs_in.at[slot], diffs_send.at[i], diffs_recv.at[slot],
            device_id={"samp": peers[i]}, device_id_type=MESH,
        )

    for i in range(3):
        diffs_copy(i, samp).start()
    diffs_in[samp] = diffs[...]
    for slot in range(4):
        @pl.when(samp != slot)
        def _(slot=slot):
            diffs_copy(0, slot).wait_recv()

    inside = lax.broadcasted_iota(jnp.int32, (1, diffs.shape[1]), 1) < rows
    level = [diffs_in[slot][0:1, :] for slot in range(4)]
    summed = level[0] + level[1] + level[2] + level[3]
    center = jnp.sum(jnp.where(inside, summed, 0.0), axis=1, keepdims=True) / (4 * rows)
    squares = [jnp.where(inside, (one - center) * (one - center), 0.0) for one in level]
    spread = jnp.sum(squares[0] + squares[1] + squares[2] + squares[3], axis=1, keepdims=True) / (4 * rows)
    standardized = (diffs[0:1, :] - center) / jnp.sqrt(spread + 1e-06)
    result_ref[...] = standardized[:, 0:rows]

    for i in range(3):
        coef_copy(i).wait_send()
        diffs_copy(i, samp).wait_send()
    for i in (0, 2):
        coef_relay(i).wait_send()

    @pl.when(is_end)
    def _():
        for i in range(len(group)):
            parts_copy(i, mine).wait_send()

    def drain(j, carry):
        core_copy(j).wait_send()
        wide, final = is_wide(j), place(j) == last

        @pl.when(jnp.logical_not(wide) | final)
        def _():
            cross_copy(j).wait_send()

        @pl.when(jnp.logical_not(wide) & (place(j) < last))
        def _():
            line_copy(j, 0).wait_send()

        @pl.when(wide & (place(j) < last))
        def _():
            line_copy(j, 1).wait_send()

        return carry

    lax.fori_loop(0, chunks, drain, 0)


JOIN_LAG, CROSS_LAG, LINE_LAG, WIDE_LAG = 2, 4, 3, 5


def lined(points, coefficients, panels, mean_field, load):
    rows = coefficients.shape[0]
    depth, own = panels.shape
    chunks = own // WIDTH
    every = pl.BlockSpec(memory_space=pl.ANY)
    here = pl.BlockSpec(memory_space=pltpu.VMEM)
    dma = pltpu.SemaphoreType.DMA
    f32 = jnp.float32
    length, sides = lax.axis_size("mode"), lax.axis_size("pts")
    padded = pl.cdiv(rows, LANES) * LANES
    result = pl.pallas_call(
        functools.partial(kernel, depth, chunks, points),
        out_shape=jax.ShapeDtypeStruct((1, rows), f32),
        in_specs=[every, every, here, here],
        out_specs=here,
        scratch_shapes=[
            pltpu.VMEM((padded, LANES), f32),
            pltpu.VMEM((8, padded), f32),
            pltpu.VMEM((2 * sides, 8, padded), f32),
            pltpu.VMEM((8, padded), f32),
            pltpu.VMEM((4, 8, padded), f32),
            pltpu.VMEM((4 * rows, depth), jnp.bfloat16),
            pltpu.VMEM((2, depth, WIDTH), jnp.bfloat16),
            pltpu.VMEM((chunks, 4 * rows, WIDTH), f32),
            pltpu.VMEM((chunks, 2 * rows, WIDTH), f32),
            pltpu.VMEM((chunks, rows, WIDTH), f32),
            pltpu.VMEM((chunks, 2 * rows, WIDTH), f32),
            dma((3,)), dma((3,)), dma, dma((2,)),
            dma((chunks,)), dma((chunks,)), dma((chunks,)), dma((chunks,)), dma((chunks,)), dma((chunks,)),
            dma((length * sides - 1,)), dma((2 * sides,)), dma((3,)), dma((4,)), dma((2,)), dma((2,)),
        ],
        compiler_params=pltpu.CompilerParams(
            collective_id=0, has_side_effects=True, vmem_limit_bytes=67043328
        ),
    )(coefficients, panels, mean_field[None, :], load[None, :])
    return result[0]


def gathered(points, coefficients, panels, mean_field, load):
    rows = lax.all_gather(coefficients, "samp", axis=0, tiled=True)
    mine = lax.all_to_all(panels, "samp", split_axis=1, concat_axis=0, tiled=True)
    partial_value = jnp.dot(rows, mine, preferred_element_type=jnp.float32)
    portion = lax.psum_scatter(partial_value, "mode", scatter_dimension=1, tiled=True)
    count = portion.shape[1]
    offset = lax.axis_index("samp") * mine.shape[1] + lax.axis_index("mode") * count
    local_mean = lax.dynamic_slice_in_dim(mean_field, offset, count, 0)
    local_load = lax.dynamic_slice_in_dim(load, offset, count, 0)
    weighted = local_load[None, :] * jnp.exp(portion + local_mean[None, :])
    even = (lax.broadcasted_iota(jnp.int32, (1, count), 1) % 2) == 0
    fine = jnp.sum(weighted, axis=1)
    coarse = jnp.sum(jnp.where(even, weighted, 0.0), axis=1)
    fine, coarse = lax.psum((fine, coarse), ("mode", "samp", "pts"))
    level_diff = fine / points - coarse * (2.0 / points)
    total = level_diff.shape[0]
    center = jnp.sum(level_diff) / total
    shifted = level_diff - center
    spread = jnp.sum(shifted * shifted) / total
    out = shifted / jnp.sqrt(spread + 1e-06)
    own = coefficients.shape[0]
    return lax.dynamic_slice_in_dim(out, lax.axis_index("samp") * own, own, 0)


def solution(mesh):
    in_specs = (P("samp", "mode"), P(("mode", "samp"), "pts"), P("pts"), P("pts"))

    def run(coefficients, panels, mean_field, load):
        def inner(*args):
            form = lined if mesh.shape["samp"] == 4 and mesh.shape["pts"] == 2 and mesh.shape["mode"] > 2 else gathered
            return form(mean_field.shape[0], *args)

        return jax.shard_map(inner, mesh=mesh, in_specs=in_specs, out_specs=P("samp"), check_vma=False)(
            coefficients, panels, mean_field, load
        )

    return run
```

```python
import functools

import jax
import jax.numpy as jnp
from jax import lax
from jax.experimental import pallas as pl
from jax.experimental.pallas import tpu as pltpu
from jax.sharding import PartitionSpec as P

MESH = pl.DeviceIdType.MESH
WIDTH = 128
PERIOD, WIDE = 2, 1
TAIL = 8
LANES = 128


def kernel(
    depth, chunks, points, coef_hbm, panel_hbm, mean_ref, load_ref, result_ref,
    acc_ref, parts, parts_in, diffs, diffs_in, coef, panel, out, core_in, cross_in, line_in,
    coef_send, coef_recv, coef_local, panel_sem,
    core_send, core_recv, cross_send, cross_recv, line_send, line_recv,
    parts_send, parts_recv, diffs_send, diffs_recv, relay_send, relay_recv,
):
    samp, line = lax.axis_index("samp"), lax.axis_index("mode")
    length = lax.axis_size("mode")
    last = length - 1
    rows = coef_hbm.shape[0]
    partner = samp + 1 - 2 * lax.rem(samp, 2)
    across = lax.rem(samp + 2, 4)
    diagonal = lax.rem(partner + 2, 4)
    peers = (across, partner, diagonal)

    barrier = pltpu.get_barrier_semaphore()
    for peer in peers:
        pl.semaphore_signal(barrier, inc=1, device_id={"samp": peer}, device_id_type=MESH)
    side, sides = lax.axis_index("pts"), lax.axis_size("pts")
    group = []
    for on in range(length * sides):
        if on > 0:
            group.append((lax.rem(line + on // sides, length), lax.rem(side + on % sides, sides)))
    for there, beside in group:
        pl.semaphore_signal(barrier, inc=1, device_id={"mode": there, "pts": beside}, device_id_type=MESH)
    pl.semaphore_wait(barrier, 3 + len(group))

    def panel_copy(j):
        slot = lax.rem(j, 2)
        columns = pl.ds(pl.multiple_of(j * WIDTH, WIDTH), WIDTH)
        return pltpu.make_async_copy(panel_hbm.at[:, columns], panel.at[slot], panel_sem.at[slot])

    half = rows // 2
    mine_half = pl.multiple_of(side * half, half)

    def coef_copy(i):
        columns = pl.ds(pl.multiple_of(peers[i] * depth, depth), depth)
        first, count = (0, rows) if i == 1 else (mine_half, half)
        return pltpu.make_async_remote_copy(
            coef_hbm.at[pl.ds(first, count), columns], coef.at[pl.ds((i + 1) * rows + first, count), :],
            coef_send.at[i], coef_recv.at[i], device_id={"samp": peers[i]}, device_id_type=MESH,
        )

    def coef_relay(i):
        block = coef.at[pl.ds((i + 1) * rows + mine_half, half), :]
        return pltpu.make_async_remote_copy(
            block, block, relay_send.at[i // 2], relay_recv.at[i // 2],
            device_id={"pts": 1 - side}, device_id_type=MESH,
        )

    for i in (0, 2, 1):
        coef_copy(i).start()
    own = pltpu.make_async_copy(
        coef_hbm.at[:, pl.ds(pl.multiple_of(samp * depth, depth), depth)], coef.at[pl.ds(0, rows), :], coef_local
    )
    own.start()
    panel_copy(0).start()
    acc_ref[...] = jnp.zeros_like(acc_ref)

    def core_copy(j):
        return pltpu.make_async_remote_copy(
            out.at[j, pl.ds(2 * rows, 2 * rows), :], core_in.at[j],
            core_send.at[j], core_recv.at[j], device_id={"samp": partner}, device_id_type=MESH,
        )

    def cross_copy(j):
        return pltpu.make_async_remote_copy(
            out.at[j, pl.ds(rows, rows), :], cross_in.at[j],
            cross_send.at[j], cross_recv.at[j], device_id={"samp": across}, device_id_type=MESH,
        )

    def up(j):
        return lax.rem(j // PERIOD, 2)

    def is_wide(j):
        return (lax.rem(j, PERIOD) >= PERIOD - WIDE) & (j < chunks - TAIL)

    def place(j):
        return up(j) * line + (1 - up(j)) * (last - line)

    def line_copy(j, kind):
        size = (1 + kind) * rows
        target = lax.rem(line + 2 * up(j) - 1 + length, length)
        return pltpu.make_async_remote_copy(
            out.at[j, pl.ds(0, size), :], line_in.at[j, pl.ds(0, size), :],
            line_send.at[j], line_recv.at[j], device_id={"mode": target}, device_id_type=MESH,
        )

    def finish(j, field):
        columns = pl.ds(pl.multiple_of(j * WIDTH, WIDTH), WIDTH)
        weighted = load_ref[:, columns] * jnp.exp(field + mean_ref[:, columns])
        total = acc_ref[pl.ds(0, rows), :]
        for at in range(0, WIDTH, LANES):
            total = total + weighted[:, at : at + LANES]
        acc_ref[pl.ds(0, rows), :] = total

    def begin(j):
        @pl.when(j + 1 < chunks)
        def _():
            panel_copy(j + 1).start()

        panel_copy(j).wait()
        out[j] = jnp.dot(coef[...], panel[lax.rem(j, 2)], preferred_element_type=jnp.float32)
        core_copy(j).start()

    def joined(j):
        core_copy(j).wait_recv()
        out[j, pl.ds(0, 2 * rows), :] += core_in[j]

        @pl.when(jnp.logical_not(is_wide(j)))
        def _():
            cross_copy(j).start()

        @pl.when(is_wide(j) & (place(j) == 0))
        def _():
            line_copy(j, 1).start()

    def crossed(j):
        cross_copy(j).wait_recv()
        out[j, pl.ds(0, rows), :] += cross_in[j]

        @pl.when(place(j) == 0)
        def _():
            line_copy(j, 0).start()

    def hop(j, kind, at):
        @pl.when(place(j) == at)
        def _():
            line_copy(j, kind).wait_recv()
            if at < last:
                out[j, pl.ds(0, (1 + kind) * rows), :] += line_in[j, pl.ds(0, (1 + kind) * rows), :]
                line_copy(j, kind).start()
            elif kind:
                out[j, pl.ds(0, 2 * rows), :] += line_in[j]
                cross_copy(j).start()
            else:
                finish(j, out[j, pl.ds(0, rows), :] + line_in[j, pl.ds(0, rows), :])

    def back(j):
        @pl.when(place(j) == last)
        def _():
            cross_copy(j).wait_recv()
            finish(j, out[j, pl.ds(0, rows), :] + cross_in[j])

    own.wait()
    for i in (0, 2):
        coef_copy(i).wait_recv()
        coef_relay(i).start()
    coef_copy(1).wait_recv()
    for i in (0, 2):
        coef_relay(i).wait_recv()

    stages = [(0, None, begin), (JOIN_LAG, None, joined), (JOIN_LAG + CROSS_LAG, 0, crossed)]
    for at in range(1, last + 1):
        stages.append((JOIN_LAG + CROSS_LAG + LINE_LAG * at, 0, functools.partial(hop, kind=0, at=at)))
        stages.append((JOIN_LAG + WIDE_LAG * at, 1, functools.partial(hop, kind=1, at=at)))
    stages.append((JOIN_LAG + WIDE_LAG * last + CROSS_LAG, 1, back))
    end = max(lag for lag, _, _ in stages)

    def tick(t, carry):
        for lag, kind, stage in stages:
            j = t - lag
            here = (j >= 0) & (j < chunks)
            if kind is not None:
                wide = is_wide(j)
                here = here & (wide if kind else jnp.logical_not(wide))
            pl.when(here)(functools.partial(stage, j))
        return carry

    lax.fori_loop(0, chunks + end, tick, 0)

    per_lane = acc_ref[...].T
    even = lax.rem(lax.broadcasted_iota(jnp.int32, per_lane.shape, 0), 2) == 0
    fine_part = jnp.sum(per_lane, axis=0, keepdims=True)
    coarse_part = jnp.sum(jnp.where(even, per_lane, 0.0), axis=0, keepdims=True)
    sublane = lax.broadcasted_iota(jnp.int32, parts.shape, 0)
    parts[...] = jnp.where(sublane == 0, fine_part, jnp.where(sublane == 1, coarse_part, 0.0))
    is_end = (line == 0) | (line == last)
    mine = (line // last) * sides + side

    def parts_copy(i, slot):
        there, beside = group[i]
        return pltpu.make_async_remote_copy(
            parts, parts_in.at[slot], parts_send.at[i], parts_recv.at[slot],
            device_id={"mode": there, "pts": beside}, device_id_type=MESH,
        )

    @pl.when(is_end)
    def _():
        for i in range(len(group)):
            parts_copy(i, mine).start()
        parts_in[mine] = parts[...]

    for slot in range(2 * sides):
        @pl.when(jnp.logical_not(is_end & (mine == slot)))
        def _(slot=slot):
            parts_copy(0, slot).wait_recv()

    total = parts_in[0]
    for slot in range(1, 2 * sides):
        total = total + parts_in[slot]
    fine, coarse = total[0:1, :] / points, total[1:2, :] * (2.0 / points)
    diffs[...] = jnp.broadcast_to(fine - coarse, diffs.shape)

    def diffs_copy(i, slot):
        return pltpu.make_async_remote_copy(
            diffs, diffs_in.at[slot], diffs_send.at[i], diffs_recv.at[slot],
            device_id={"samp": peers[i]}, device_id_type=MESH,
        )

    for i in range(3):
        diffs_copy(i, samp).start()
    diffs_in[samp] = diffs[...]
    for slot in range(4):
        @pl.when(samp != slot)
        def _(slot=slot):
            diffs_copy(0, slot).wait_recv()

    inside = lax.broadcasted_iota(jnp.int32, (1, diffs.shape[1]), 1) < rows
    level = [diffs_in[slot][0:1, :] for slot in range(4)]
    summed = level[0] + level[1] + level[2] + level[3]
    center = jnp.sum(jnp.where(inside, summed, 0.0), axis=1, keepdims=True) / (4 * rows)
    squares = [jnp.where(inside, (one - center) * (one - center), 0.0) for one in level]
    spread = jnp.sum(squares[0] + squares[1] + squares[2] + squares[3], axis=1, keepdims=True) / (4 * rows)
    standardized = (diffs[0:1, :] - center) / jnp.sqrt(spread + 1e-06)
    result_ref[...] = standardized[:, 0:rows]

    for i in range(3):
        coef_copy(i).wait_send()
        diffs_copy(i, samp).wait_send()
    for i in (0, 2):
        coef_relay(i).wait_send()

    @pl.when(is_end)
    def _():
        for i in range(len(group)):
            parts_copy(i, mine).wait_send()

    def drain(j, carry):
        core_copy(j).wait_send()
        wide, final = is_wide(j), place(j) == last

        @pl.when(jnp.logical_not(wide) | final)
        def _():
            cross_copy(j).wait_send()

        @pl.when(jnp.logical_not(wide) & (place(j) < last))
        def _():
            line_copy(j, 0).wait_send()

        @pl.when(wide & (place(j) < last))
        def _():
            line_copy(j, 1).wait_send()

        return carry

    lax.fori_loop(0, chunks, drain, 0)


JOIN_LAG, CROSS_LAG, LINE_LAG, WIDE_LAG = 2, 4, 3, 5


def lined(points, coefficients, panels, mean_field, load):
    rows = coefficients.shape[0]
    depth, own = panels.shape
    chunks = own // WIDTH
    every = pl.BlockSpec(memory_space=pl.ANY)
    here = pl.BlockSpec(memory_space=pltpu.VMEM)
    dma = pltpu.SemaphoreType.DMA
    f32 = jnp.float32
    length, sides = lax.axis_size("mode"), lax.axis_size("pts")
    padded = pl.cdiv(rows, LANES) * LANES
    result = pl.pallas_call(
        functools.partial(kernel, depth, chunks, points),
        out_shape=jax.ShapeDtypeStruct((1, rows), f32),
        in_specs=[every, every, here, here],
        out_specs=here,
        scratch_shapes=[
            pltpu.VMEM((padded, LANES), f32),
            pltpu.VMEM((8, padded), f32),
            pltpu.VMEM((2 * sides, 8, padded), f32),
            pltpu.VMEM((8, padded), f32),
            pltpu.VMEM((4, 8, padded), f32),
            pltpu.VMEM((4 * rows, depth), jnp.bfloat16),
            pltpu.VMEM((2, depth, WIDTH), jnp.bfloat16),
            pltpu.VMEM((chunks, 4 * rows, WIDTH), f32),
            pltpu.VMEM((chunks, 2 * rows, WIDTH), f32),
            pltpu.VMEM((chunks, rows, WIDTH), f32),
            pltpu.VMEM((chunks, 2 * rows, WIDTH), f32),
            dma((3,)), dma((3,)), dma, dma((2,)),
            dma((chunks,)), dma((chunks,)), dma((chunks,)), dma((chunks,)), dma((chunks,)), dma((chunks,)),
            dma((length * sides - 1,)), dma((2 * sides,)), dma((3,)), dma((4,)), dma((2,)), dma((2,)),
        ],
        compiler_params=pltpu.CompilerParams(
            collective_id=0, has_side_effects=True, vmem_limit_bytes=67043328
        ),
    )(coefficients, panels, mean_field[None, :], load[None, :])
    return result[0]


def gathered(points, coefficients, panels, mean_field, load):
    rows = lax.all_gather(coefficients, "samp", axis=0, tiled=True)
    mine = lax.all_to_all(panels, "samp", split_axis=1, concat_axis=0, tiled=True)
    partial_value = jnp.dot(rows, mine, preferred_element_type=jnp.float32)
    portion = lax.psum_scatter(partial_value, "mode", scatter_dimension=1, tiled=True)
    count = portion.shape[1]
    offset = lax.axis_index("samp") * mine.shape[1] + lax.axis_index("mode") * count
    local_mean = lax.dynamic_slice_in_dim(mean_field, offset, count, 0)
    local_load = lax.dynamic_slice_in_dim(load, offset, count, 0)
    weighted = local_load[None, :] * jnp.exp(portion + local_mean[None, :])
    even = (lax.broadcasted_iota(jnp.int32, (1, count), 1) % 2) == 0
    fine = jnp.sum(weighted, axis=1)
    coarse = jnp.sum(jnp.where(even, weighted, 0.0), axis=1)
    fine, coarse = lax.psum((fine, coarse), ("mode", "samp", "pts"))
    level_diff = fine / points - coarse * (2.0 / points)
    total = level_diff.shape[0]
    center = jnp.sum(level_diff) / total
    shifted = level_diff - center
    spread = jnp.sum(shifted * shifted) / total
    out = shifted / jnp.sqrt(spread + 1e-06)
    own = coefficients.shape[0]
    return lax.dynamic_slice_in_dim(out, lax.axis_index("samp") * own, own, 0)


def solution(mesh):
    in_specs = (P("samp", "mode"), P(("mode", "samp"), "pts"), P("pts"), P("pts"))

    def run(coefficients, panels, mean_field, load):
        def inner(*args):
            form = lined if mesh.shape["samp"] == 4 and mesh.shape["pts"] == 2 and mesh.shape["mode"] > 2 else gathered
            return form(mean_field.shape[0], *args)

        return jax.shard_map(inner, mesh=mesh, in_specs=in_specs, out_specs=P("samp"), check_vma=False)(
            coefficients, panels, mean_field, load
        )

    return run
```
